256 devices in a mesh: freq: 32 (over x, y, core), mode: 8 (over z).
Axes of the slice: x: 4, y: 4, z: 8, core: 2. Of those that a mesh axis runs over, the one named last changes fastest.
Arguments:
- excitation: bfloat16 [16, 2, 1024, 2048], P(None, None, 'freq', 'mode'), may hold values from -6 to 6
- coupling: bfloat16 [3, 32, 2, 2048, 2048], P(None, 'freq', None, 'mode'), may hold values from -3 to 3, as said below
- wavenumber: float32 [1024, 2048], P('freq', 'mode'), may hold values from 0.02 to 0.2
- mode_counts: int32 [1024], P('freq'), may hold values from 128 to 2048, as said below
- seg_steps: int32 [3], replicated, may hold values from 8 to 64
- shapes: bfloat16 [32, 2048, 512], P('freq'), may hold values from -0.125 to 0.125
- spectrum: float32 [2, 1024], P(None, 'freq'), may hold values from -6 to 6
Outputs:
- traces: float32 [16, 512, 4096], P('mode', 'freq')
The draws below stay inside these ranges and needn't reach their ends.
Inputs may be any that keep to these rules, and one draw needn't show every extreme that they name: `mode_counts`: each count is a multiple of 128; counts tend to rise with frequency; the first frequency has 128 modes and the last has all 2048. `coupling`: the real part of each matrix is near the identity on its diagonal; all entries are independent otherwise.
All inputs are finite; a program needn't handle non-finite values.
Results may differ from the reference program's by a relative error of at most 0.015.
Values may be sent and summed in bfloat16 or wider, within the bound.
No kernel may reach another device: no remote copies, remote signals or barrier semaphores. Data moves between devices by JAX's collectives and lax.ppermute only.
A program may use at most 128 MiB of HBM per device.

```python
import math
import jax
import jax.numpy as jnp
from jax import lax

M = 2048
MODE_BLOCK = 128
SEG = 3
SRC = 16
R = 512
NT = 4096
FREQ_DEV = 32
BANDS = 32
NF = 1024
K0 = 64


def draw_coupling(key, part):
    full_shape = (SEG, BANDS, 2, M, M)
    noise_key = jax.random.fold_in(jax.random.fold_in(key, 17), 0)
    noise_part = jax.random.normal(noise_key, full_shape, jnp.float32)
    diagonal = jnp.ones((SEG, BANDS, 1, M, 1), jnp.float32)
    real_only = (jnp.arange(2) == 0).astype(jnp.float32).reshape(1, 1, 2, 1, 1)
    identity = jnp.eye(M, dtype=jnp.float32)
    matrix = real_only * diagonal * identity + noise_part * (0.4 / math.sqrt(M))
    return matrix.astype(jnp.bfloat16)


def draw_mode_counts(key, part):
    blocks = M // MODE_BLOCK
    position = jnp.arange(NF, dtype=jnp.int32)
    rising = 1 + (blocks - 1) * position // max(NF - 1, 1)
    jitter = jax.random.randint(jax.random.fold_in(key, 29), (NF,), -1, 2, dtype=jnp.int32)
    counts = jnp.clip(rising + jitter, 1, blocks)
    counts = jnp.where(position == 0, 1, jnp.where(position == NF - 1, blocks, counts))
    return (counts * MODE_BLOCK).astype(jnp.int32)


def block_scale(rng, dims, pieces, low, largest):
    loudness, own = 1.0, jax.random.fold_in(rng, 6)
    for axis_at, shards_of in pieces:
        draws = jnp.exp(jax.random.uniform(jax.random.fold_in(own, axis_at), (shards_of,), jnp.float32, low / len(pieces), largest / len(pieces)))
        loudness = loudness * jnp.repeat(draws, dims[axis_at] // shards_of).reshape([-1 if axis == axis_at else 1 for axis in range(len(dims))])
    return loudness


def noise(key, extent, scale, reach, shards=(), kind=jnp.bfloat16):
    loudness = block_scale(key, extent, shards, -0.22, 0.18) if shards else 1.0
    entries = jax.random.normal(key, extent, jnp.float32) * scale * loudness
    return jnp.minimum(jnp.maximum(entries, -reach), reach).astype(kind)


def setup_inputs(seed: int = 0) -> dict:
    keys = jax.random.split(jax.random.key(seed), 8)
    return {
        "excitation": noise(keys[0], (SRC, 2, NF, M), 1.0, 6.0, ((2, 32), (3, 8))),
        "coupling": draw_coupling(jax.random.fold_in(keys[7], 71), 0),
        "wavenumber": jnp.clip(0.02 + 0.18 * jax.random.uniform(keys[2], (NF, M), jnp.float32) ** block_scale(keys[2], (NF, M), ((0, 32), (1, 8)), -0.2, 0.2), 0.02, 0.2),
        "mode_counts": draw_mode_counts(jax.random.fold_in(keys[7], 71), 0),
        "seg_steps": jax.random.randint(keys[4], (SEG,), 8, 65).astype(jnp.int32),
        "shapes": noise(keys[5], (BANDS, M, R), M ** -0.5, 0.125, ((0, 32),)),
        "spectrum": noise(keys[6], (2, NF), 1.0, 6.0, ((1, 32),), jnp.float32),
    }


def make_table(first_bin, count):
    freq_index = first_bin + jnp.arange(count, dtype=jnp.int32)
    sample = jnp.arange(NT, dtype=jnp.int32)
    phase_step = (freq_index[:, None] + K0) * sample[None, :] % NT
    angles = phase_step.astype(jnp.float32) * (2.0 * math.pi / NT)
    return jnp.stack([jnp.cos(angles), -jnp.sin(angles)], axis=0).astype(jnp.bfloat16)

def propagate_band(band, excitation, coupling, wavenumber, mode_counts, seg_steps, shapes, spectrum):
    lowest = (band * FREQ_DEV).astype(jnp.int32)
    source_part = lax.dynamic_slice_in_dim(excitation, lowest, FREQ_DEV, 2)
    phase_rate = lax.dynamic_slice_in_dim(wavenumber, lowest, FREQ_DEV, 0)
    counts = lax.dynamic_slice_in_dim(mode_counts, lowest, FREQ_DEV, 0)
    living = (jnp.arange(M, dtype=jnp.int32)[None, :] < counts[:, None]).astype(jnp.float32)
    amplitude = (source_part.astype(jnp.float32) * living).astype(jnp.bfloat16)
    for segment in range(SEG):
        matrix = lax.dynamic_index_in_dim(coupling[segment], band, 0, keepdims=False)
        stacked = matrix.reshape(2 * M, M)
        product = jnp.dot(amplitude.reshape(SRC * 2 * FREQ_DEV, M), stacked.T, preferred_element_type=jnp.float32)
        product = product.reshape(SRC, 2, FREQ_DEV, 2, M)
        coupled_real = product[:, 0, :, 0] - product[:, 1, :, 1]
        coupled_imaginary = product[:, 1, :, 0] + product[:, 0, :, 1]
        angles = phase_rate * seg_steps[segment].astype(jnp.float32)
        factor_real = living * jnp.cos(angles)
        factor_imaginary = living * jnp.sin(angles)
        amplitude = jnp.stack([coupled_real * factor_real - coupled_imaginary * factor_imaginary, coupled_real * factor_imaginary + coupled_imaginary * factor_real], axis=1).astype(jnp.bfloat16)
    mode_shapes = lax.dynamic_index_in_dim(shapes, band, 0, keepdims=False)
    field = jnp.dot(amplitude.reshape(SRC * 2 * FREQ_DEV, M), mode_shapes, preferred_element_type=jnp.float32)
    field = field.reshape(SRC, 2, FREQ_DEV, R)
    weights = lax.dynamic_slice_in_dim(spectrum, lowest, FREQ_DEV, 1)
    weight_real = weights[0][None, :, None]
    weight_imaginary = weights[1][None, :, None]
    weighted = jnp.stack([weight_real * field[:, 0] - weight_imaginary * field[:, 1], weight_real * field[:, 1] + weight_imaginary * field[:, 0]], axis=1)
    return weighted.astype(jnp.bfloat16)

def reference(excitation, coupling, wavenumber, mode_counts, seg_steps, shapes, spectrum):

    def one_band(band):
        return propagate_band(band, excitation, coupling, wavenumber, mode_counts, seg_steps, shapes, spectrum)
    every_band = lax.map(one_band, jnp.arange(BANDS, dtype=jnp.int32))
    weighted = jnp.transpose(every_band, (1, 2, 0, 3, 4)).reshape(SRC, 2, NF, R)
    table = make_table(0, NF)
    summed = jnp.einsum('scfr,cft->srt', weighted.astype(jnp.float32), table.astype(jnp.float32))
    return summed * (1.0 / math.sqrt(NF))
```

```python
import functools
import math

import jax
import jax.numpy as jnp
import numpy as np
from jax import lax
from jax.experimental import pallas as pl
from jax.experimental.pallas import tpu as pltpu
from jax.sharding import PartitionSpec as P

NT = 4096
T1 = 128
T2 = NT // T1


def transform_tables(bands, local, first_bin):
    base = first_bin // local
    t1 = np.arange(T1)[:, None]
    turn = 2.0 * np.pi * (((np.arange(bands)[None, :] + base) * t1 * local) % NT) / NT
    outer = np.concatenate([np.cos(turn), np.sin(turn)], axis=1)
    lane_l = np.tile(np.arange(local), 4)[None, :]
    twist = 2.0 * np.pi * ((lane_l * t1) % NT) / NT
    lane = np.arange(4 * local)
    lane_s, lane_c = lane // (2 * local), (lane // local) % 2
    row = np.arange(2 * T2)[:, None]
    row_s, row_t2 = row // T2, row % T2
    spin = 2.0 * np.pi * ((lane_l * row_t2 * T1) % NT) / NT
    inner = np.where(lane_c[None, :] == 0, np.cos(spin), -np.sin(spin))
    inner = np.where(lane_s[None, :] == row_s, inner, 0.0) / math.sqrt(bands * local)
    return (
        jnp.asarray(outer, jnp.bfloat16),
        jnp.asarray(np.cos(twist), jnp.float32),
        jnp.asarray(np.sin(twist), jnp.float32),
        jnp.asarray(inner, jnp.bfloat16),
    )


def transform_kernel(bands, local, receivers, x_ref, outer_ref, cos_ref, sin_ref, inner_ref, out_ref, wide, tall):
    x = x_ref[...].astype(jnp.float32)
    lanes = lax.broadcasted_iota(jnp.int32, x.shape, 1)
    first = (lanes // local) % 2 == 0
    ahead = pltpu.roll(x, 3 * local, 1)
    behind = pltpu.roll(x, local, 1)
    rows = x.shape[0]
    wide[0:rows] = x
    wide[rows : 2 * rows] = jnp.where(first, -ahead, behind)
    for r in range(receivers):
        straight = wide[pl.ds(r, bands, stride=receivers), :]
        turned = wide[pl.ds(rows + r, bands, stride=receivers), :]
        top = jnp.concatenate([straight, turned], axis=1)
        low = jnp.concatenate([turned, -straight], axis=1)
        both = jnp.concatenate([top, low], axis=0).astype(jnp.bfloat16)
        stage = jnp.dot(outer_ref[...], both, preferred_element_type=jnp.float32)
        twisted = stage[:, : 4 * local] * cos_ref[...] + stage[:, 4 * local :] * sin_ref[...]
        tall[pl.ds(r, 2 * T2, stride=receivers), :] = lax.dot_general(
            inner_ref[...],
            twisted.astype(jnp.bfloat16),
            (((1,), (1,)), ((), ())),
            preferred_element_type=jnp.float32,
        )
    for s in range(2):
        for t2 in range(T2):
            start = (s * T2 + t2) * receivers
            out_ref[s, :, t2 * T1 : (t2 + 1) * T1] = tall[start : start + receivers, :]


def transform(x, bands, local, receivers, first_bin):
    tables = transform_tables(bands, local, first_bin)
    return pl.pallas_call(
        functools.partial(transform_kernel, bands, local, receivers),
        out_shape=jax.ShapeDtypeStruct((2, receivers, NT), jnp.float32),
        scratch_shapes=[
            pltpu.VMEM((2 * bands * receivers, 4 * local), jnp.float32),
            pltpu.VMEM((2 * T2 * receivers, T1), jnp.float32),
        ],
        cost_estimate=pl.CostEstimate(flops=200_000_000, bytes_accessed=1_000_000, transcendentals=0),
        name="transform",
    )(x, *tables)


def couple_kernel(offsets, width, bins, here_ref, matrix_ref, real_ref, imaginary_ref, *refs):
    shards, out_ref = refs[:-1], refs[-1]
    planes = len(shards)
    total = None
    for offset, shard in zip(offsets, shards):
        column = lax.rem(here_ref[0] + (offset + planes), planes) * width
        piece = matrix_ref[0, 0, :, :, pl.ds(pl.multiple_of(column, width), width)]
        term = lax.dot_general(
            shard[...],
            piece.reshape(2 * width, width),
            (((1,), (1,)), ((), ())),
            preferred_element_type=jnp.float32,
        )
        total = term if total is None else total + term
    factor_real, factor_imaginary = real_ref[...], imaginary_ref[...]
    for s in range(total.shape[0] // (2 * bins)):
        top = total[(2 * s) * bins : (2 * s + 1) * bins]
        low = total[(2 * s + 1) * bins : (2 * s + 2) * bins]
        real = top[:, :width] - low[:, width:]
        imaginary = low[:, :width] + top[:, width:]
        out_ref[(2 * s) * bins : (2 * s + 1) * bins] = (
            real * factor_real - imaginary * factor_imaginary
        ).astype(out_ref.dtype)
        out_ref[(2 * s + 1) * bins : (2 * s + 2) * bins] = (
            real * factor_imaginary + imaginary * factor_real
        ).astype(out_ref.dtype)


def couple(here, coupling, segment, factors, offsets, shards, bins):
    rows, width = shards[0].shape
    flops = 4 * rows * width * width * len(shards)

    def whole(*shape):
        return pl.BlockSpec(shape, lambda i: (0,) * len(shape))

    return pl.pallas_call(
        functools.partial(couple_kernel, offsets, width, bins),
        grid=(1,),
        in_specs=[
            pl.BlockSpec(memory_space=pltpu.SMEM),
            pl.BlockSpec((1,) + coupling.shape[1:], lambda i: (segment, 0, 0, 0, 0)),
        ]
        + [whole(bins, width)] * 2
        + [whole(rows, width)] * len(shards),
        out_specs=whole(rows, width),
        out_shape=jax.ShapeDtypeStruct((rows, width), jnp.bfloat16),
        cost_estimate=pl.CostEstimate(flops=flops, bytes_accessed=5_000_000, transcendentals=0),
        name="couple",
    )(here, coupling, *factors, *shards)


def field_kernel(even_ref, odd_ref, shapes_ref, out_ref):
    planes, _, width = even_ref.shape
    total = None
    for p in range(planes):
        rows = jnp.concatenate([even_ref[p], odd_ref[p]], axis=0)
        term = jnp.dot(
            rows, shapes_ref[p * width : (p + 1) * width, :], preferred_element_type=jnp.float32
        )
        total = term if total is None else total + term
    out_ref[...] = total.T.astype(out_ref.dtype)


def field(even, odd, mode_shapes):
    rows = 2 * even.shape[1]
    receivers = mode_shapes.shape[1]
    return pl.pallas_call(
        field_kernel,
        out_shape=jax.ShapeDtypeStruct((receivers, rows), jnp.bfloat16),
        cost_estimate=pl.CostEstimate(flops=270_000_000, bytes_accessed=3_000_000, transcendentals=0),
        name="field",
    )(even, odd, mode_shapes)


def gather_ring(mine, planes, more_up):
    up = [(i, (i + 1) % planes) for i in range(planes)]
    down = [(i, (i - 1) % planes) for i in range(planes)]
    steps = planes // 2
    offsets, shards = [0], [mine]
    rising = falling = mine
    for step in range(1, steps + 1):
        if step < steps or more_up:
            rising = lax.ppermute(rising, "mode", up)
            offsets.append(-step)
            shards.append(rising)
        if step < steps or not more_up:
            falling = lax.ppermute(falling, "mode", down)
            offsets.append(step)
            shards.append(falling)
    return offsets, shards


def shards(excitation, coupling, wavenumber, mode_counts, seg_steps, shapes, spectrum):
    sources, _, bins, width = excitation.shape
    planes = lax.axis_size("mode")
    bands = lax.axis_size("freq")
    here = lax.axis_index("mode")
    mode_number = here * width + jnp.arange(width, dtype=jnp.int32)
    living = (mode_number[None, :] < mode_counts[:, None]).astype(jnp.float32)
    masked = (excitation.astype(jnp.float32) * living).astype(jnp.bfloat16)
    masked = masked.reshape(planes, sources // planes, 2 * bins, width)
    chains = [masked[:, s].reshape(planes * 2 * bins, width) for s in range(2)]
    here = here.astype(jnp.int32).reshape(1)
    segments = coupling.shape[0]
    for segment in range(segments):
        angles = wavenumber * seg_steps[segment].astype(jnp.float32)
        factor_real, factor_imaginary = living * jnp.cos(angles), living * jnp.sin(angles)
        if segment == segments - 1:
            weight_real, weight_imaginary = spectrum[0][:, None], spectrum[1][:, None]
            factor_real, factor_imaginary = (
                weight_real * factor_real - weight_imaginary * factor_imaginary,
                weight_real * factor_imaginary + weight_imaginary * factor_real,
            )
        gathered = [gather_ring(chain, planes, s == 0) for s, chain in enumerate(chains)]
        chains = [
            couple(here, coupling, segment, (factor_real, factor_imaginary), offsets, blocks, bins)
            for offsets, blocks in gathered
        ]
    even, odd = [
        lax.all_to_all(
            chain.reshape(planes, 2 * bins, width), "mode", split_axis=0, concat_axis=0, tiled=True
        )
        for chain in chains
    ]
    weighted = field(even, odd, shapes[0])
    weighted = lax.all_to_all(weighted, "freq", split_axis=0, concat_axis=0, tiled=True)
    all_bins = bins * bands
    return transform(weighted, bands, bins, weighted.shape[0] // bands, all_bins // 16)


def solution(mesh):
    in_specs = (
        P(None, None, "freq", "mode"),
        P(None, "freq", None, "mode", None),
        P("freq", "mode"),
        P("freq"),
        P(),
        P("freq", None, None),
        P(None, "freq"),
    )
    out_specs = P("mode", "freq", None)
    return jax.shard_map(shards, mesh=mesh, in_specs=in_specs, out_specs=out_specs, check_vma=False)
```

```python
import functools
import math

import jax
import jax.numpy as jnp
import numpy as np
from jax import lax
from jax.experimental import pallas as pl
from jax.experimental.pallas import tpu as pltpu
from jax.sharding import PartitionSpec as P

NT = 4096
T1 = 128
T2 = NT // T1


def transform_tables(bands, local, first_bin):
    base = first_bin // local
    t1 = np.arange(T1)[:, None]
    turn = 2.0 * np.pi * (((np.arange(bands)[None, :] + base) * t1 * local) % NT) / NT
    outer = np.concatenate([np.cos(turn), np.sin(turn)], axis=1)
    lane_l = np.tile(np.arange(local), 4)[None, :]
    twist = 2.0 * np.pi * ((lane_l * t1) % NT) / NT
    lane = np.arange(4 * local)
    lane_s, lane_c = lane // (2 * local), (lane // local) % 2
    row = np.arange(2 * T2)[:, None]
    row_s, row_t2 = row // T2, row % T2
    spin = 2.0 * np.pi * ((lane_l * row_t2 * T1) % NT) / NT
    inner = np.where(lane_c[None, :] == 0, np.cos(spin), -np.sin(spin))
    inner = np.where(lane_s[None, :] == row_s, inner, 0.0) / math.sqrt(bands * local)
    return (
        jnp.asarray(outer, jnp.bfloat16),
        jnp.asarray(np.cos(twist), jnp.float32),
        jnp.asarray(np.sin(twist), jnp.float32),
        jnp.asarray(inner, jnp.bfloat16),
    )


def transform_kernel(bands, local, receivers, x_ref, outer_ref, cos_ref, sin_ref, inner_ref, out_ref, wide, tall):
    x = x_ref[...].astype(jnp.float32)
    lanes = lax.broadcasted_iota(jnp.int32, x.shape, 1)
    first = (lanes // local) % 2 == 0
    ahead = pltpu.roll(x, 3 * local, 1)
    behind = pltpu.roll(x, local, 1)
    rows = x.shape[0]
    wide[0:rows] = x
    wide[rows : 2 * rows] = jnp.where(first, -ahead, behind)
    def receiver(r):
        straight = wide[pl.ds(r, bands, stride=receivers), :]
        turned = wide[pl.ds(rows + r, bands, stride=receivers), :]
        top = jnp.concatenate([straight, turned], axis=1)
        low = jnp.concatenate([turned, -straight], axis=1)
        both = jnp.concatenate([top, low], axis=0).astype(jnp.bfloat16)
        stage = jnp.dot(outer_ref[...], both, preferred_element_type=jnp.float32)
        twisted = stage[:, : 4 * local] * cos_ref[...] + stage[:, 4 * local :] * sin_ref[...]
        tall[pl.ds(r, 2 * T2, stride=receivers), :] = lax.dot_general(
            inner_ref[...],
            twisted.astype(jnp.bfloat16),
            (((1,), (1,)), ((), ())),
            preferred_element_type=jnp.float32,
        )

    def some(n, carry):
        for r in range(4):
            receiver(4 * n + r)
        return carry

    lax.fori_loop(0, receivers // 4, some, 0)
    for s in range(2):
        for t2 in range(T2):
            start = (s * T2 + t2) * receivers
            out_ref[s, :, t2 * T1 : (t2 + 1) * T1] = tall[start : start + receivers, :]


def transform(x, bands, local, receivers, first_bin):
    tables = transform_tables(bands, local, first_bin)
    return pl.pallas_call(
        functools.partial(transform_kernel, bands, local, receivers),
        out_shape=jax.ShapeDtypeStruct((2, receivers, NT), jnp.float32),
        scratch_shapes=[
            pltpu.VMEM((2 * bands * receivers, 4 * local), jnp.float32),
            pltpu.VMEM((2 * T2 * receivers, T1), jnp.float32),
        ],
        cost_estimate=pl.CostEstimate(flops=200_000_000, bytes_accessed=1_000_000, transcendentals=0),
        name="transform",
    )(x, *tables)


def couple_kernel(first, last, offsets, planes, bins, here_ref, matrix_ref, *refs):
    refs = list(refs)
    shards = [refs.pop(0) for _ in offsets]
    carried = None if first else refs.pop(0)
    factors = [refs.pop(0) for _ in range(2)] if last else None
    out_ref, rows_buffer, matrix_buffer, rows_sem, matrix_sem = refs[:5]
    total_ref = refs[5] if last else out_ref
    rows, width = rows_buffer.shape[1:]
    copies = []
    position, segment = here_ref[0], here_ref[1]
    sign = 1 - 2 * lax.rem(position, 2)
    for i, (offset, shard) in enumerate(zip(offsets, shards)):
        column = lax.rem(position + sign * offset + planes, planes) * width
        piece = matrix_ref.at[segment, 0, :, :, pl.ds(pl.multiple_of(column, width), width)]
        pair = (
            pltpu.make_async_copy(piece, matrix_buffer.at[i], matrix_sem.at[i]),
            pltpu.make_async_copy(shard, rows_buffer.at[i], rows_sem.at[i]),
        )
        for copy in pair:
            copy.start()
        copies.append(pair)
    block = 2 * bins

    def add(i):
        term = lax.dot_general(
            rows_buffer[i],
            matrix_buffer[i].reshape(2 * width, width),
            (((1,), (1,)), ((), ())),
            preferred_element_type=jnp.float32,
        )
        return term

    if first:
        total_ref[...] = jnp.zeros_like(total_ref)
        start = 0
    else:
        for copy in copies[0]:
            copy.wait()
        total_ref[...] = carried[...] + add(0)
        start = 1

    def step(i, carry):
        pltpu.make_async_copy(matrix_buffer.at[i], matrix_buffer.at[i], matrix_sem.at[i]).wait()
        pltpu.make_async_copy(rows_buffer.at[i], rows_buffer.at[i], rows_sem.at[i]).wait()
        total_ref[...] += add(i)
        return carry

    if start < len(copies):
        lax.fori_loop(start, len(copies), step, 0)
    if last:
        factor_real, factor_imaginary = factors[0][...], factors[1][...]

        def rotate(s, carry):
            top = total_ref[pl.ds(pl.multiple_of(s * block, block), bins), :]
            low = total_ref[pl.ds(pl.multiple_of(s * block + bins, bins), bins), :]
            real = top[:, :width] - low[:, width:]
            imaginary = low[:, :width] + top[:, width:]
            out_ref[pl.ds(pl.multiple_of(s * block, block), bins), :] = (
                real * factor_real - imaginary * factor_imaginary
            ).astype(out_ref.dtype)
            out_ref[pl.ds(pl.multiple_of(s * block + bins, bins), bins), :] = (
                real * factor_imaginary + imaginary * factor_real
            ).astype(out_ref.dtype)
            return carry

        lax.fori_loop(0, rows // block, rotate, 0)


def couple_part(here, coupling, planes, offsets, shards, bins, carried=None, factors=None):
    first, last = carried is None, factors is not None
    rows, width = shards[0].shape
    n = len(shards)
    anywhere = pl.BlockSpec(memory_space=pl.ANY)
    vmem = pl.BlockSpec(memory_space=pltpu.VMEM)
    operands = [here, coupling, *shards] + ([] if first else [carried]) + (list(factors) if last else [])
    in_hbm = pl.BlockSpec(memory_space=pltpu.HBM)
    specs = [pl.BlockSpec(memory_space=pltpu.SMEM), in_hbm] + [anywhere] * n
    specs += [vmem] * (len(operands) - len(specs))
    scratch = [
        pltpu.VMEM((n, rows, width), jnp.bfloat16),
        pltpu.VMEM((n, 2, width, width), jnp.bfloat16),
        pltpu.SemaphoreType.DMA((n,)),
        pltpu.SemaphoreType.DMA((n,)),
    ]
    if last:
        scratch.append(pltpu.VMEM((rows, 2 * width), jnp.float32))
        out = jax.ShapeDtypeStruct((rows, width), jnp.bfloat16)
    else:
        out = jax.ShapeDtypeStruct((rows, 2 * width), jnp.float32)
    return pl.pallas_call(
        functools.partial(couple_kernel, first, last, offsets, planes, bins),
        in_specs=specs,
        out_specs=vmem,
        out_shape=out,
        scratch_shapes=scratch,
        compiler_params=pltpu.CompilerParams(vmem_limit_bytes=12 << 20),
        cost_estimate=pl.CostEstimate(
            flops=4 * rows * width * width * n, bytes_accessed=600_000 * n, transcendentals=0
        ),
        name="couple_last" if last else "couple_first",
    )(*operands)


def couple(here, coupling, factors, offsets, shards, bins):
    planes = len(shards)
    part = couple_part(here, coupling, planes, offsets[:-1], shards[:-1], bins)
    return couple_part(
        here, coupling, planes, offsets[-1:], shards[-1:], bins, carried=part, factors=factors
    )


def field_kernel(even_ref, odd_ref, shapes_ref, out_ref):
    planes, _, width = even_ref.shape
    total = None
    for p in range(planes):
        rows = jnp.concatenate([even_ref[p], odd_ref[p]], axis=0)
        term = jnp.dot(
            rows, shapes_ref[p * width : (p + 1) * width, :], preferred_element_type=jnp.float32
        )
        total = term if total is None else total + term
    out_ref[...] = total.T.astype(out_ref.dtype)


def field(even, odd, mode_shapes):
    rows = 2 * even.shape[1]
    receivers = mode_shapes.shape[1]
    return pl.pallas_call(
        field_kernel,
        out_shape=jax.ShapeDtypeStruct((receivers, rows), jnp.bfloat16),
        cost_estimate=pl.CostEstimate(flops=270_000_000, bytes_accessed=3_000_000, transcendentals=0),
        name="field",
    )(even, odd, mode_shapes)


def gather_swaps(mine, planes, even_last):
    even = [(i, i ^ 1) for i in range(planes)]
    odd = [(i, (i - 1) % planes if i % 2 == 0 else (i + 1) % planes) for i in range(planes)]
    steps = planes // 2
    offsets, shards = [0], [mine]
    over_even = over_odd = mine
    for step in range(1, steps + 1):
        to_even, to_odd = over_odd, over_even
        if step < steps or even_last:
            over_even = lax.ppermute(to_even, "mode", even)
            offsets.append(step)
            shards.append(over_even)
        if step < steps or not even_last:
            over_odd = lax.ppermute(to_odd, "mode", odd)
            offsets.append(-step if step < steps else step)
            shards.append(over_odd)
    return offsets, shards


def shards(excitation, coupling, wavenumber, mode_counts, seg_steps, shapes, spectrum):
    sources, _, bins, width = excitation.shape
    planes = lax.axis_size("mode")
    bands = lax.axis_size("freq")
    here = lax.axis_index("mode")
    mode_number = here * width + jnp.arange(width, dtype=jnp.int32)
    living = (mode_number[None, :] < mode_counts[:, None]).astype(jnp.float32)
    masked = (excitation.astype(jnp.float32) * living).astype(jnp.bfloat16)
    masked = masked.reshape(planes, sources // planes, 2 * bins, width)
    chains = [masked[:, s].reshape(planes * 2 * bins, width) for s in range(2)]
    here = here.astype(jnp.int32)
    segments = coupling.shape[0]
    angles = wavenumber[None] * seg_steps.astype(jnp.float32)[:, None, None]
    factor_real, factor_imaginary = living * jnp.cos(angles), living * jnp.sin(angles)
    weight_real, weight_imaginary = spectrum[0][:, None], spectrum[1][:, None]
    for segment in range(segments):
        factors = factor_real[segment], factor_imaginary[segment]
        if segment == segments - 1:
            factors = (
                weight_real * factors[0] - weight_imaginary * factors[1],
                weight_real * factors[1] + weight_imaginary * factors[0],
            )
        where = jnp.stack([here, jnp.int32(segment)])
        gathered = [gather_swaps(chain, planes, s == 0) for s, chain in enumerate(chains)]
        chains = [
            couple(where, coupling, factors, offsets, blocks, bins)
            for offsets, blocks in gathered
        ]
    even, odd = [
        lax.all_to_all(
            chain.reshape(planes, 2 * bins, width), "mode", split_axis=0, concat_axis=0, tiled=True
        )
        for chain in chains
    ]
    weighted = field(even, odd, shapes[0])
    weighted = lax.all_to_all(weighted, "freq", split_axis=0, concat_axis=0, tiled=True)
    all_bins = bins * bands
    return transform(weighted, bands, bins, weighted.shape[0] // bands, all_bins // 16)


def solution(mesh):
    in_specs = (
        P(None, None, "freq", "mode"),
        P(None, "freq", None, "mode", None),
        P("freq", "mode"),
        P("freq"),
        P(),
        P("freq", None, None),
        P(None, "freq"),
    )
    out_specs = P("mode", "freq", None)
    return jax.shard_map(shards, mesh=mesh, in_specs=in_specs, out_specs=out_specs, check_vma=False)
```

```python
import functools
import math

import jax
import jax.numpy as jnp
import numpy as np
from jax import lax
from jax.experimental import pallas as pl
from jax.experimental.pallas import tpu as pltpu
from jax.sharding import PartitionSpec as P


NT = 4096
T1 = 128
T2 = NT // T1


def transform_tables(bands, local, first_bin):
    base = first_bin // local
    t1 = np.arange(T1)[:, None]
    turn = 2.0 * np.pi * (((np.arange(bands)[None, :] + base) * t1 * local) % NT) / NT
    outer = np.concatenate([np.cos(turn), np.sin(turn)], axis=1)
    lane_l = np.tile(np.arange(local), 4)[None, :]
    twist = 2.0 * np.pi * ((lane_l * t1) % NT) / NT
    lane = np.arange(4 * local)
    lane_s, lane_c = lane // (2 * local), (lane // local) % 2
    row = np.arange(2 * T2)[:, None]
    row_s, row_t2 = row // T2, row % T2
    spin = 2.0 * np.pi * ((lane_l * row_t2 * T1) % NT) / NT
    inner = np.where(lane_c[None, :] == 0, np.cos(spin), -np.sin(spin))
    inner = np.where(lane_s[None, :] == row_s, inner, 0.0) / math.sqrt(bands * local)
    return (
        jnp.asarray(outer, jnp.bfloat16),
        jnp.asarray(np.cos(twist), jnp.float32),
        jnp.asarray(np.sin(twist), jnp.float32),
        jnp.asarray(inner, jnp.bfloat16),
    )


def transform_kernel(bands, local, receivers, x_ref, outer_ref, cos_ref, sin_ref, inner_ref, out_ref, wide, tall):
    x = x_ref[...].astype(jnp.float32)
    lanes = lax.broadcasted_iota(jnp.int32, x.shape, 1)
    first = (lanes // local) % 2 == 0
    ahead = pltpu.roll(x, 3 * local, 1)
    behind = pltpu.roll(x, local, 1)
    rows = x.shape[0]
    wide[0:rows] = x
    wide[rows : 2 * rows] = jnp.where(first, -ahead, behind)

    def receiver(r):
        straight = wide[pl.ds(r, bands, stride=receivers), :]
        turned = wide[pl.ds(rows + r, bands, stride=receivers), :]
        top = jnp.concatenate([straight, turned], axis=1)
        low = jnp.concatenate([turned, -straight], axis=1)
        both = jnp.concatenate([top, low], axis=0).astype(jnp.bfloat16)
        stage = jnp.dot(outer_ref[...], both, preferred_element_type=jnp.float32)
        twisted = stage[:, : 4 * local] * cos_ref[...] + stage[:, 4 * local :] * sin_ref[...]
        tall[pl.ds(r, 2 * T2, stride=receivers), :] = lax.dot_general(
            inner_ref[...],
            twisted.astype(jnp.bfloat16),
            (((1,), (1,)), ((), ())),
            preferred_element_type=jnp.float32,
        )

    def some(n, carry):
        for r in range(8):
            receiver(8 * n + r)
        return carry

    lax.fori_loop(0, receivers // 8, some, 0)
    for s in range(2):
        for t2 in range(T2):
            start = (s * T2 + t2) * receivers
            out_ref[s, :, t2 * T1 : (t2 + 1) * T1] = tall[start : start + receivers, :]


def transform(x, bands, local, receivers, first_bin):
    tables = transform_tables(bands, local, first_bin)
    return pl.pallas_call(
        functools.partial(transform_kernel, bands, local, receivers),
        out_shape=jax.ShapeDtypeStruct((2, receivers, NT), jnp.float32),
        scratch_shapes=[
            pltpu.VMEM((2 * bands * receivers, 4 * local), jnp.float32),
            pltpu.VMEM((2 * T2 * receivers, T1), jnp.float32),
        ],
        cost_estimate=pl.CostEstimate(flops=200_000_000, bytes_accessed=1_000_000, transcendentals=0),
        name="transform",
    )(x, *tables)


def couple_kernel(first, last, joins, offsets, planes, bins, here_ref, matrix_ref, *refs):
    refs = list(refs)
    shards = [refs.pop(0) for _ in offsets]
    carried = None if first else refs.pop(0)
    factors = [refs.pop(0) for _ in range(2)] if last else None
    other = refs.pop(0) if joins else None
    out_ref, rows_buffer, matrix_buffer, rows_sem, matrix_sem = refs[:5]
    total_ref = refs[5] if last else out_ref
    rows, width = rows_buffer.shape[1:]
    copies = []
    position, segment = here_ref[0], here_ref[1]
    sign = 1 - 2 * lax.rem(position, 2)
    for i, (offset, shard) in enumerate(zip(offsets, shards)):
        column = lax.rem(position + sign * offset + planes, planes) * width
        piece = matrix_ref.at[segment, 0, :, :, pl.ds(pl.multiple_of(column, width), width)]
        pair = (
            pltpu.make_async_copy(piece, matrix_buffer.at[i], matrix_sem.at[i]),
            pltpu.make_async_copy(shard, rows_buffer.at[i], rows_sem.at[i]),
        )
        for copy in pair:
            copy.start()
        copies.append(pair)
    block = 2 * bins

    def add(i):
        term = lax.dot_general(
            rows_buffer[i],
            matrix_buffer[i].reshape(2 * width, width),
            (((1,), (1,)), ((), ())),
            preferred_element_type=jnp.float32,
        )
        return term

    if first:
        total_ref[...] = jnp.zeros_like(total_ref)
        start = 0
    else:
        for copy in copies[0]:
            copy.wait()
        total_ref[...] = carried[...] + add(0)
        start = 1

    def step(i, carry):
        pltpu.make_async_copy(matrix_buffer.at[i], matrix_buffer.at[i], matrix_sem.at[i]).wait()
        pltpu.make_async_copy(rows_buffer.at[i], rows_buffer.at[i], rows_sem.at[i]).wait()
        total_ref[...] += add(i)
        return carry

    if start < len(copies):
        lax.fori_loop(start, len(copies), step, 0)
    if last:
        factor_real, factor_imaginary = factors[0][...], factors[1][...]

        def rotate(s, carry):
            top = total_ref[pl.ds(pl.multiple_of(s * block, block), bins), :]
            low = total_ref[pl.ds(pl.multiple_of(s * block + bins, bins), bins), :]
            real = top[:, :width] - low[:, width:]
            imaginary = low[:, :width] + top[:, width:]
            turned_real = (real * factor_real - imaginary * factor_imaginary).astype(out_ref.dtype)
            turned_imaginary = (real * factor_imaginary + imaginary * factor_real).astype(out_ref.dtype)
            if joins:
                out_ref[s, 0:block, :] = other[pl.ds(pl.multiple_of(s * block, block), block), :]
                out_ref[s, block : block + bins, :] = turned_real
                out_ref[s, block + bins : 2 * block, :] = turned_imaginary
            else:
                out_ref[pl.ds(pl.multiple_of(s * block, block), bins), :] = turned_real
                out_ref[pl.ds(pl.multiple_of(s * block + bins, bins), bins), :] = turned_imaginary
            return carry

        lax.fori_loop(0, rows // block, rotate, 0)


def couple_part(here, coupling, planes, offsets, shards, bins, carried=None, factors=None, other=None):
    first, last, joins = carried is None, factors is not None, other is not None
    rows, width = shards[0].shape
    n = len(shards)
    anywhere = pl.BlockSpec(memory_space=pl.ANY)
    vmem = pl.BlockSpec(memory_space=pltpu.VMEM)
    operands = [here, coupling, *shards] + ([] if first else [carried]) + (list(factors) if last else []) + ([other] if joins else [])
    in_hbm = pl.BlockSpec(memory_space=pltpu.HBM)
    specs = [pl.BlockSpec(memory_space=pltpu.SMEM), in_hbm] + [anywhere] * n
    specs += [vmem] * (len(operands) - len(specs))
    scratch = [
        pltpu.VMEM((n, rows, width), jnp.bfloat16),
        pltpu.VMEM((n, 2, width, width), jnp.bfloat16),
        pltpu.SemaphoreType.DMA((n,)),
        pltpu.SemaphoreType.DMA((n,)),
    ]
    if last:
        scratch.append(pltpu.VMEM((rows, 2 * width), jnp.float32))
        out = jax.ShapeDtypeStruct((rows, width), jnp.bfloat16)
        if joins:
            block = 2 * bins
            out = jax.ShapeDtypeStruct((rows // block, 2 * block, width), jnp.bfloat16)
    else:
        out = jax.ShapeDtypeStruct((rows, 2 * width), jnp.float32)
    return pl.pallas_call(
        functools.partial(couple_kernel, first, last, joins, offsets, planes, bins),
        in_specs=specs,
        out_specs=vmem,
        out_shape=out,
        scratch_shapes=scratch,
        compiler_params=pltpu.CompilerParams(vmem_limit_bytes=12 << 20),
        cost_estimate=pl.CostEstimate(
            flops=4 * rows * width * width * n, bytes_accessed=600_000 * n, transcendentals=0
        ),
        name="couple_join" if joins else "couple_last" if last else "couple_first",
    )(*operands)


def couple_first(here, coupling, offsets, shards, bins):
    return couple_part(here, coupling, len(shards), offsets[:-1], shards[:-1], bins)


def couple_last(here, coupling, factors, offsets, shards, bins, part, other=None):
    return couple_part(
        here, coupling, len(shards), offsets[-1:], shards[-1:], bins, part, factors, other
    )


def field_kernel(rows_ref, shapes_ref, out_ref):
    planes, _, width = rows_ref.shape
    total = None
    for p in range(planes):
        term = jnp.dot(
            rows_ref[p], shapes_ref[p * width : (p + 1) * width, :], preferred_element_type=jnp.float32
        )
        total = term if total is None else total + term
    out_ref[...] = total.T.astype(out_ref.dtype)


def field(rows, mode_shapes):
    receivers = mode_shapes.shape[1]
    return pl.pallas_call(
        field_kernel,
        out_shape=jax.ShapeDtypeStruct((receivers, rows.shape[1]), jnp.bfloat16),
        cost_estimate=pl.CostEstimate(flops=270_000_000, bytes_accessed=3_000_000, transcendentals=0),
        name="field",
    )(rows, mode_shapes)


def gather_swaps(mine, planes, even_last):
    even = [(i, i ^ 1) for i in range(planes)]
    odd = [(i, (i - 1) % planes if i % 2 == 0 else (i + 1) % planes) for i in range(planes)]
    steps = planes // 2
    offsets, shards = [0], [mine]
    over_even = over_odd = mine
    for step in range(1, steps + 1):
        to_even, to_odd = over_odd, over_even
        if step < steps or even_last:
            over_even = lax.ppermute(to_even, "mode", even)
            offsets.append(step)
            shards.append(over_even)
        if step < steps or not even_last:
            over_odd = lax.ppermute(to_odd, "mode", odd)
            offsets.append(-step if step < steps else step)
            shards.append(over_odd)
    return offsets, shards


def shards(excitation, coupling, wavenumber, mode_counts, seg_steps, shapes, spectrum):
    sources, _, bins, width = excitation.shape
    planes = lax.axis_size("mode")
    bands = lax.axis_size("freq")
    here = lax.axis_index("mode")
    mode_number = here * width + jnp.arange(width, dtype=jnp.int32)
    living = (mode_number[None, :] < mode_counts[:, None]).astype(jnp.float32)
    masked = (excitation.astype(jnp.float32) * living).astype(jnp.bfloat16)
    masked = masked.reshape(planes, sources // planes, 2 * bins, width)
    chains = [masked[:, s].reshape(planes * 2 * bins, width) for s in range(2)]
    here = here.astype(jnp.int32)
    coupling = pltpu.with_memory_space_constraint(coupling, pltpu.HBM)
    segments = coupling.shape[0]
    angles = wavenumber[None] * seg_steps.astype(jnp.float32)[:, None, None]
    factor_real, factor_imaginary = living * jnp.cos(angles), living * jnp.sin(angles)
    weight_real, weight_imaginary = spectrum[0][:, None], spectrum[1][:, None]
    for segment in range(segments):
        factors = factor_real[segment], factor_imaginary[segment]
        if segment == segments - 1:
            factors = (
                weight_real * factors[0] - weight_imaginary * factors[1],
                weight_real * factors[1] + weight_imaginary * factors[0],
            )
        where = jnp.stack([here, jnp.int32(segment)])
        gathered = [gather_swaps(chain, planes, s == 0) for s, chain in enumerate(chains)]
        parts = [couple_first(where, coupling, *gathered[s], bins) for s in range(2)]
        ahead = couple_last(where, coupling, factors, *gathered[0], bins, parts[0])
        other = ahead if segment == segments - 1 else None
        behind = couple_last(where, coupling, factors, *gathered[1], bins, parts[1], other)
        chains = [ahead, behind]
    owned = lax.all_to_all(behind, "mode", split_axis=0, concat_axis=0, tiled=True)
    weighted = field(owned, shapes[0])
    weighted = lax.all_to_all(weighted, "freq", split_axis=0, concat_axis=0, tiled=True)
    all_bins = bins * bands
    return transform(weighted, bands, bins, weighted.shape[0] // bands, all_bins // 16)


def solution(mesh):
    in_specs = (
        P(None, None, "freq", "mode"),
        P(None, "freq", None, "mode", None),
        P("freq", "mode"),
        P("freq"),
        P(),
        P("freq", None, None),
        P(None, "freq"),
    )
    out_specs = P("mode", "freq", None)

    return jax.shard_map(shards, mesh=mesh, in_specs=in_specs, out_specs=out_specs, check_vma=False)
```
